768 devices in a mesh: section: 4 (over x), dp: 16 (over y, z_hi), tensor: 12 (over z_lo, core).
Axes of the slice: x: 4, y: 8, z: 12 (z_hi: 2, z_lo: 6; z = z_hi * 6 + z_lo), core: 2. Of those that a mesh axis runs over, the one named last changes fastest.
Arguments:
- enc_hidden: bfloat16 [16, 1152, 4096], P('dp', 'section'), may hold values from -6 to 6
- dec_hidden: bfloat16 [4, 16, 192, 4096], P('section', 'dp', 'tensor'), may hold values from -6 to 6
- enc_gain: bfloat16 [4096], replicated, may hold values from 0.25 to 1.75
- dec_gain: bfloat16 [4, 4096], P('section'), may hold values from 0.25 to 1.75
- w_query: bfloat16 [4, 4096, 3072], P('section', None, 'tensor'), may hold values from -0.0234375 to 0.0234375
- w_key: bfloat16 [4, 4096, 3072], P('section', None, 'tensor'), may hold values from -0.09375 to 0.09375
- w_value: bfloat16 [4, 4096, 3072], P('section', None, 'tensor'), may hold values from -0.09375 to 0.09375
- w_out: bfloat16 [4, 3072, 4096], P('section', 'tensor'), may hold values from -0.109375 to 0.109375
Outputs:
- cross_out: bfloat16 [4, 16, 192, 4096], P('section', 'dp', 'tensor')
The draws below stay inside these ranges and needn't reach their ends.
All inputs are finite; a program needn't handle non-finite values.
Results may differ from the reference program's by a relative error of at most 0.017.
Values may be sent and summed in bfloat16 or wider, within the bound.
A program may use at most 64 MiB of HBM per device.

```python
import jax
import jax.numpy as jnp
from jax import lax

D = 4096
HD = 256
HEADS = 12
SEQS = 16
ENC_LEN = 1152
DEC_LEN = 192
N_SECTION = 4


def shard_levels(key, extent, cuts, low, high):
    level, own = 1.0, jax.random.fold_in(key, 6)
    for dim, parts in cuts:
        steps = jnp.exp(jax.random.uniform(jax.random.fold_in(own, dim), (parts,), jnp.float32, low / len(cuts), high / len(cuts)))
        level = level * jnp.repeat(steps, extent[dim] // parts).reshape([-1 if axis == dim else 1 for axis in range(len(extent))])
    return level


def scatter_about(rng, shape, width, bound, shards=(), held_as=jnp.bfloat16):
    array = jax.random.normal(rng, shape, jnp.float32) * width
    if len(shards) > 0:
        array = shard_levels(rng, shape, shards, -0.22, 0.18) * array
    return jnp.clip(array, min=-bound, max=bound).astype(held_as)


def setup_inputs(seed: int = 0) -> dict:
    arg_keys = jax.random.split(jax.random.key(seed), 9)
    enc_hidden = scatter_about(arg_keys[0], (SEQS, ENC_LEN, D), 1.0, 6.0, ((0, 16), (1, 4)))
    dec_hidden = scatter_about(arg_keys[1], (N_SECTION, SEQS, DEC_LEN, D), 1.0, 6.0, ((0, 4), (1, 16), (2, 12)))
    enc_gain = jnp.clip(1.0 + 0.15 * jax.random.normal(arg_keys[2], (D,), jnp.float32), 0.25, 1.75).astype(jnp.bfloat16)
    dec_gain = jnp.clip(1.0 + 0.15 * jax.random.normal(arg_keys[3], (N_SECTION, D), jnp.float32), 0.25, 1.75).astype(jnp.bfloat16)
    w_query = scatter_about(arg_keys[4], (N_SECTION, D, HEADS * HD), (16 * D) ** -0.5, 0.0234375, ((0, 4), (2, 12)))
    w_key = scatter_about(arg_keys[5], (N_SECTION, D, HEADS * HD), D ** -0.5, 0.09375, ((0, 4), (2, 12)))
    w_value = scatter_about(arg_keys[6], (N_SECTION, D, HEADS * HD), D ** -0.5, 0.09375, ((0, 4), (2, 12)))
    w_out = scatter_about(arg_keys[7], (N_SECTION, HEADS * HD, D), (HEADS * HD) ** -0.5, 0.109375, ((0, 4), (1, 12)))
    return {"enc_hidden": enc_hidden, "dec_hidden": dec_hidden, "enc_gain": enc_gain, "dec_gain": dec_gain, "w_query": w_query, "w_key": w_key, "w_value": w_value, "w_out": w_out}


def normalize(hidden, gain):
    values = hidden.astype(jnp.float32)
    mean_sq = lax.optimization_barrier(jnp.mean(values * values, axis=-1, keepdims=True))
    return (values * lax.rsqrt(mean_sq + 1e-06) * gain.astype(jnp.float32)).astype(jnp.bfloat16)

def reference(enc_hidden, dec_hidden, enc_gain, dec_gain, w_query, w_key, w_value, w_out):
    memory = normalize(enc_hidden, enc_gain)

    def layer(operands):
        hidden, gain, wq_layer, wk_layer, wv_layer, wo_layer = operands

        def one_sequence(pair):
            mem_rows, dec_rows = pair
            normed = normalize(dec_rows, gain)
            queries = jnp.dot(normed, wq_layer, preferred_element_type=jnp.float32).astype(jnp.bfloat16)
            keys = jnp.dot(mem_rows, wk_layer, preferred_element_type=jnp.float32).astype(jnp.bfloat16)
            values = jnp.dot(mem_rows, wv_layer, preferred_element_type=jnp.float32).astype(jnp.bfloat16)
            queries = queries.reshape(queries.shape[0], HEADS, HD).astype(jnp.float32)
            keys = keys.reshape(keys.shape[0], HEADS, HD).astype(jnp.float32)
            values = values.reshape(values.shape[0], HEADS, HD).astype(jnp.float32)
            scores = jnp.einsum('qhd,khd->hqk', queries, keys)
            exponent = jnp.exp(scores)
            attention = (exponent / lax.optimization_barrier(jnp.sum(exponent, axis=-1, keepdims=True))).astype(jnp.bfloat16)
            attended = jnp.einsum('hqk,khd->qhd', attention.astype(jnp.float32), values).astype(jnp.bfloat16)
            attended = attended.reshape(attended.shape[0], HEADS * HD)
            return jnp.dot(attended, wo_layer, preferred_element_type=jnp.float32).astype(jnp.bfloat16)
        return lax.map(one_sequence, (memory, hidden))
    return lax.map(layer, (dec_hidden, dec_gain, w_query, w_key, w_value, w_out))
```

```python
import functools

import jax
import jax.numpy as jnp
from jax import lax
from jax.experimental import pallas as pl
from jax.experimental.pallas import tpu as pltpu
from jax.sharding import PartitionSpec as P

F32 = jnp.float32
BF16 = jnp.bfloat16
MESH = pl.DeviceIdType.MESH

EX = 32
B1 = 16
B2 = 32
SHARED = B1 + 2 * B2
SPLIT = 2


def kernel(
    chips,
    enc_ref,
    dec_ref,
    enc_gain_ref,
    dec_gain_ref,
    wq_ref,
    wk_ref,
    wv_ref,
    wo_ref,
    out_ref,
    mem,
    dec,
    wq,
    wkv,
    wo,
    rms,
    dec_rms,
    kv,
    expo,
    part,
    to_core,
    from_core,
    to_line,
    from_line,
    send_sems,
    local_sems,
    x_sems,
    z_sems,
    core_sems,
    dec_sems,
    dec_core_sems,
    pair_sems,
    line_sems,
    line_send_sems,
):
    sections = lax.axis_size("section")
    s = lax.axis_index("section")
    t = lax.axis_index("tensor")
    z = t // 2
    c = t % 2
    e = z % 2
    last = chips - 1
    width = mem.shape[2]
    section_up = {"section": lax.rem(s + 1, sections)}
    section_down = {"section": lax.rem(s + sections - 1, sections)}
    other_core = {"tensor": t + 1 - 2 * c}
    z_partner = {"tensor": t + 2 - 4 * e}
    z_up = {"tensor": t + 2}
    z_down = {"tensor": t - 2}

    barrier = pltpu.get_barrier_semaphore()
    for target in (section_up, section_down, other_core):
        pl.semaphore_signal(barrier, inc=1, device_id=target, device_id_type=MESH)

    @pl.when(z < last)
    def _():
        pl.semaphore_signal(barrier, inc=1, device_id=z_up, device_id_type=MESH)

    @pl.when(z > 0)
    def _():
        pl.semaphore_signal(barrier, inc=1, device_id=z_down, device_id_type=MESH)

    locals_ = [
        pltpu.make_async_copy(src, dst, local_sems.at[i])
        for i, (src, dst) in enumerate(
            (
                (wk_ref.at[0], wkv.at[0]),
                (wv_ref.at[0], wkv.at[1]),
                (wq_ref.at[0], wq),
                (enc_ref.at[0], mem.at[0]),
                (dec_ref.at[0, 0], dec.at[t]),
                (wo_ref.at[0], wo),
            )
        )
    ]
    for copy in locals_:
        copy.start()

    pl.semaphore_wait(barrier, 3 + (z < last).astype(jnp.int32) + (z > 0).astype(jnp.int32))

    pending = []

    def send(src, dst, recv_sem, target, when=None):
        copy = pltpu.make_async_remote_copy(
            src_ref=src,
            dst_ref=dst,
            send_sem=send_sems.at[len(pending)],
            recv_sem=recv_sem,
            device_id=target,
            device_id_type=MESH,
        )
        pending.append((copy, when))
        if when is None:
            copy.start()
        else:
            pl.when(when)(copy.start)

    def arrived(dst, recv_sem):
        pltpu.make_async_remote_copy(
            src_ref=dst,
            dst_ref=dst,
            send_sem=send_sems.at[0],
            recv_sem=recv_sem,
            device_id=other_core,
            device_id_type=MESH,
        ).wait_recv()

    def piece_rows(piece, parity, core):
        if piece == 0:
            start, size = (2 * parity + core) * EX, EX
        elif piece == 1:
            start, size = 4 * EX + core * SHARED, B1
        else:
            start, size = 4 * EX + core * SHARED + B1 + (piece - 2) * B2, B2
        return pl.ds(pl.multiple_of(start, 16), size)

    for up_piece, down_piece in ((0, 0), (2, 1), (3, 2), (1, 3)):
        send(
            enc_ref.at[0, piece_rows(up_piece, e, c)],
            mem.at[2, piece_rows(up_piece, e, c)],
            x_sems.at[2, up_piece],
            section_up,
        )
        send(
            enc_ref.at[0, piece_rows(down_piece, e, c)],
            mem.at[1, piece_rows(down_piece, e, c)],
            x_sems.at[1, down_piece],
            section_down,
        )
    send(dec_ref.at[0, 0], dec.at[t], dec_sems.at[0, 1], z_up, z < last)
    send(dec_ref.at[0, 0], dec.at[t], dec_sems.at[1, 1], z_down, z > 0)
    send(dec_ref.at[0, 0], dec.at[t], dec_core_sems.at[0, 0], other_core)

    def from_x(slot, piece):
        block = mem.at[slot, piece_rows(piece, e, c)]
        arrived(block, x_sems.at[slot, piece])
        if slot == 1 and piece in (0, 1):
            target = mem.at[3, piece_rows(piece, e, c)]
            send(block, target, x_sems.at[3, piece], section_down)
        if slot == 2 and piece in (2, 3):
            target = mem.at[3, piece_rows(piece, e, c)]
            send(block, target, x_sems.at[3, piece], section_up)
        if piece == 0:
            send(block, block, z_sems.at[slot], z_partner)
        send(block, block, core_sems.at[slot, piece], other_core)

    def from_z(slot):
        block = mem.at[slot, piece_rows(0, 1 - e, c)]
        arrived(block, z_sems.at[slot])
        send(block, block, core_sems.at[slot, 4], other_core)

    def from_core_all(slot):
        for piece in range(4):
            arrived(mem.at[slot, piece_rows(piece, e, 1 - c)], core_sems.at[slot, piece])
        arrived(mem.at[slot, piece_rows(0, 1 - e, 1 - c)], core_sems.at[slot, 4])

    def from_decoder(k):
        below = z - k >= 0
        source = dec.at[jnp.maximum(t - 2 * k, 0)]

        @pl.when(below)
        def _():
            arrived(source, dec_sems.at[0, k])

        if k < last:
            send(source, source, dec_sems.at[0, k + 1], z_up, below & (z < last))
        send(source, source, dec_core_sems.at[0, k], other_core, below)
        above = z + k <= last
        source_ = dec.at[jnp.minimum(t + 2 * k, 2 * chips - 1)]

        @pl.when(above)
        def _():
            arrived(source_, dec_sems.at[1, k])

        if k < last:
            send(source_, source_, dec_sems.at[1, k + 1], z_down, above & (z > 0))
        send(source_, source_, dec_core_sems.at[1, k], other_core, above)

    def decoder_from_core():
        arrived(dec.at[t + 1 - 2 * c], dec_core_sems.at[0, 0])
        for k in range(1, chips):

            @pl.when(z - k >= 0)
            def _():
                source = dec.at[jnp.maximum(t - 2 * k + 1 - 2 * c, 0)]
                arrived(source, dec_core_sems.at[0, k])

            @pl.when(z + k <= last)
            def _():
                source = dec.at[jnp.minimum(t + 2 * k + 1 - 2 * c, 2 * chips - 1)]
                arrived(source, dec_core_sems.at[1, k])

    def project(slot):
        def row_group(i, carry):
            rows = pl.ds(pl.multiple_of(i * 16, 16), 16)
            x = mem[slot, rows, :].astype(F32)
            mean_sq = jnp.sum(x * x, axis=-1, keepdims=True) * (1.0 / width)
            rms[rows, :] = lax.rsqrt(mean_sq + 1e-06)
            return carry

        lax.fori_loop(0, mem.shape[1] // 16, row_group, 0)

        def side(n, carry):
            projected = jnp.dot(mem[slot], wkv[n], preferred_element_type=F32)
            kv[n, slot] = (projected * rms[...]).astype(BF16)
            return carry

        lax.fori_loop(0, 2, side, 0)

    locals_[0].wait()
    locals_[1].wait()
    locals_[2].wait()

    def fold(i, carry):
        start = pl.multiple_of(i * 128, 128)
        rows = pl.ds(start, 128)
        enc_gain = jnp.broadcast_to(enc_gain_ref[:, pl.ds(start, 128)].astype(F32), (128, 128)).T
        dec_gain = jnp.broadcast_to(dec_gain_ref[:, pl.ds(start, 128)].astype(F32), (128, 128)).T
        for half in range(wq.shape[1] // 128):
            columns = pl.ds(half * 128, 128)
            for n in range(2):
                wkv[n, rows, columns] = (wkv[n, rows, columns].astype(F32) * enc_gain).astype(BF16)
            wq[rows, columns] = (wq[rows, columns].astype(F32) * dec_gain).astype(BF16)
        return carry

    lax.fori_loop(0, width // 128, fold, 0)

    from_decoder(1)
    from_x(1, 0)
    from_x(2, 0)
    from_decoder(2)
    locals_[3].wait()
    project(0)
    from_decoder(3) if chips > 3 else None
    from_x(1, 1)
    from_x(2, 2)
    from_z(1)
    from_z(2)
    from_decoder(4) if chips > 4 else None
    from_x(1, 2)
    from_x(2, 3)
    from_decoder(5) if chips > 5 else None
    locals_[4].wait()
    decoder_from_core()

    def decoder_rows(i, carry):
        x = dec[i].astype(F32)
        mean_sq = jnp.sum(x * x, axis=-1, keepdims=True) * (1.0 / width)
        dec_rms[i] = lax.rsqrt(mean_sq + 1e-06)
        return carry

    lax.fori_loop(0, 2 * chips, decoder_rows, 0)
    tokens = 2 * chips * dec.shape[1]
    queries = jnp.dot(dec[...].reshape(tokens, width), wq[...], preferred_element_type=F32)
    queries = (queries * dec_rms[...].reshape(tokens, 1)).astype(BF16)

    def score(slot):
        scores = lax.dot_general(
            queries, kv[0, slot], (((1,), (1,)), ((), ())), preferred_element_type=F32
        )
        exponent = jnp.exp(scores)
        expo[slot] = exponent
        return jnp.sum(exponent, axis=-1, keepdims=True)

    total = score(0)
    from_x(1, 3)
    from_x(2, 1)
    from_core_all(1)
    project(1)
    from_x(3, 0)
    from_core_all(2)
    project(2)
    from_x(3, 1)
    from_x(3, 2)
    total += score(1)
    total += score(2)
    from_x(3, 3)
    from_z(3)
    from_core_all(3)
    project(3)
    total += score(3)
    inverse = 1.0 / total
    attended = jnp.zeros((tokens, kv.shape[3]), F32)
    for slot in range(4):
        attention = (expo[slot] * inverse).astype(BF16)
        attended += jnp.dot(attention, kv[1, slot], preferred_element_type=F32)
    attended = attended.astype(BF16)
    locals_[5].wait()

    tile = min(512, width)
    for n in range(width // tile):
        columns = pl.ds(n * tile, tile)
        product = jnp.dot(attended, wo[:, columns], preferred_element_type=F32)
        part[:, :, columns] = product.reshape(2 * chips, dec.shape[1], tile)

    first = (z >= chips // 2).astype(jnp.int32)

    def line(direction, k):
        position = jnp.where(direction == 0, z, last - z)
        dest = jnp.where(direction == 0, last - k, k)
        return position, dest

    pair = []
    for k in range(chips):
        _, dest = line(first, k)
        to_core[dest] = part[2 * dest + 1 - c].astype(BF16)
        copy = pltpu.make_async_remote_copy(
            src_ref=to_core.at[dest],
            dst_ref=from_core.at[dest],
            send_sem=pair_sems.at[0, k],
            recv_sem=pair_sems.at[1, k],
            device_id=other_core,
            device_id_type=MESH,
        )
        copy.start()
        pair.append(copy)

    piece_width = width // SPLIT
    sent = []

    def pass_on(direction, k):
        position, dest = line(direction, k)
        active = last - k > position
        for h in range(SPLIT):
            columns = pl.ds(h * piece_width, piece_width)
            landed = from_line.at[direction, dest, h]
            copy = pltpu.make_async_remote_copy(
                src_ref=to_line.at[direction, dest, h],
                dst_ref=landed,
                send_sem=line_send_sems.at[direction, k, h],
                recv_sem=line_sems.at[direction, k, h],
                device_id={"tensor": t + 2 - 4 * direction},
                device_id_type=MESH,
            )
            own = lambda: part[2 * dest + c, :, columns] + from_core[dest, :, columns].astype(F32)

            @pl.when(active & (position == 0))
            def _():
                to_line[direction, dest, h] = own().astype(BF16)
                copy.start()

            @pl.when(active & (position > 0))
            def _():
                arrived(landed, line_sems.at[direction, k, h])
                value = own() + from_line[direction, dest, h].astype(F32)
                to_line[direction, dest, h] = value.astype(BF16)
                copy.start()

            sent.append((copy, active))

    for k in range(chips):
        pair[k].wait_recv()
        if k < last:
            pass_on(first, k)
    for k in range(last - (chips + 1) // 2):
        pass_on(1 - first, k)

    for h in range(SPLIT):
        columns = pl.ds(h * piece_width, piece_width)
        part[t, :, columns] += from_core[z, :, columns].astype(F32)

        @pl.when(z > 0)
        def _():
            arrived(from_line.at[0, z, h], line_sems.at[0, last - z, h])
            part[t, :, columns] += from_line[0, z, h].astype(F32)

        @pl.when(z < last)
        def _():
            arrived(from_line.at[1, z, h], line_sems.at[1, z, h])
            part[t, :, columns] += from_line[1, z, h].astype(F32)

        out_ref[:, columns] = part[t, :, columns].astype(BF16)

    for copy, when in pending + sent:
        if when is None:
            copy.wait_send()
        else:
            pl.when(when)(copy.wait_send)
    for copy in pair:
        copy.wait_send()


def body(enc_hidden, dec_hidden, enc_gain, dec_gain, w_query, w_key, w_value, w_out):
    chips = lax.axis_size("tensor") // 2
    rows, width = enc_hidden.shape[1:]
    share = dec_hidden.shape[2]
    head = w_query.shape[2]
    any_space = pl.BlockSpec(memory_space=pl.ANY)
    vmem = pl.BlockSpec(memory_space=pltpu.VMEM)
    dma = pltpu.SemaphoreType.DMA
    mixed = pl.pallas_call(
        functools.partial(kernel, chips),
        out_shape=jax.ShapeDtypeStruct((share, width), BF16),
        in_specs=[any_space, any_space, vmem, vmem] + [any_space] * 4,
        out_specs=vmem,
        scratch_shapes=[
            pltpu.VMEM((4, rows, width), BF16),
            pltpu.VMEM((2 * chips, share, width), BF16),
            pltpu.VMEM((width, head), BF16),
            pltpu.VMEM((2, width, head), BF16),
            pltpu.VMEM((head, width), BF16),
            pltpu.VMEM((rows, 1), F32),
            pltpu.VMEM((2 * chips, share, 1), F32),
            pltpu.VMEM((2, 4, rows, head), BF16),
            pltpu.VMEM((4, 2 * chips * share, rows), F32),
            pltpu.VMEM((2 * chips, share, width), F32),
            pltpu.VMEM((chips, share, width), BF16),
            pltpu.VMEM((chips, share, width), BF16),
            pltpu.VMEM((2, chips, SPLIT, share, width // SPLIT), BF16),
            pltpu.VMEM((2, chips, SPLIT, share, width // SPLIT), BF16),
            dma((64,)),
            dma((6,)),
            dma((4, 4)),
            dma((4,)),
            dma((4, 5)),
            dma((2, chips + 1)),
            dma((2, chips)),
            dma((2, chips)),
            dma((2, chips, SPLIT)),
            dma((2, chips, SPLIT)),
        ],
        compiler_params=pltpu.CompilerParams(
            collective_id=0, has_side_effects=True, vmem_limit_bytes=60 * 1024 * 1024
        ),
        name="cross_attention",
    )(
        enc_hidden,
        dec_hidden,
        enc_gain.reshape(1, width),
        dec_gain,
        w_query,
        w_key,
        w_value,
        w_out,
    )
    return mixed[None, None]


def solution(mesh):
    return jax.shard_map(
        body,
        mesh=mesh,
        in_specs=(
            P("dp", "section", None),
            P("section", "dp", "tensor", None),
            P(),
            P("section", None),
            P("section", None, "tensor"),
            P("section", None, "tensor"),
            P("section", None, "tensor"),
            P("section", "tensor", None),
        ),
        out_specs=P("section", "dp", "tensor", None),
        check_vma=False,
    )
```

```python
import functools

import jax
import jax.numpy as jnp
from jax import lax
from jax.experimental import pallas as pl
from jax.experimental.pallas import tpu as pltpu
from jax.sharding import PartitionSpec as P

F32 = jnp.float32
BF16 = jnp.bfloat16
MESH = pl.DeviceIdType.MESH

EX = 32
B1 = 16
B2 = 32
SHARED = B1 + 2 * B2
SPLIT = 2


def kernel(
    chips,
    enc_ref,
    dec_ref,
    enc_gain_ref,
    dec_gain_ref,
    wq_ref,
    wk_ref,
    wv_ref,
    wo_ref,
    out_ref,
    mem,
    dec,
    wq,
    wkv,
    wo,
    gain,
    query,
    total,
    kv,
    expo,
    part,
    to_core,
    from_core_rows,
    to_line,
    from_line,
    send_sems,
    local_sems,
    x_sems,
    z_sems,
    core_sems,
    dec_sems,
    dec_core_sems,
    pair_sems,
    line_sems,
    line_send_sems,
):
    sections = lax.axis_size("section")
    s = lax.axis_index("section")
    t = lax.axis_index("tensor")
    z = t // 2
    c = t % 2
    e = z % 2
    last = chips - 1
    width = mem.shape[2]
    section_up = {"section": lax.rem(s + 1, sections)}
    section_down = {"section": lax.rem(s + sections - 1, sections)}
    other_core = {"tensor": t + 1 - 2 * c}
    z_partner = {"tensor": t + 2 - 4 * e}
    z_up = {"tensor": t + 2}
    z_down = {"tensor": t - 2}

    barrier = pltpu.get_barrier_semaphore()
    for target in (section_up, section_down, other_core):
        pl.semaphore_signal(barrier, inc=1, device_id=target, device_id_type=MESH)

    @pl.when(z < last)
    def _():
        pl.semaphore_signal(barrier, inc=1, device_id=z_up, device_id_type=MESH)

    @pl.when(z > 0)
    def _():
        pl.semaphore_signal(barrier, inc=1, device_id=z_down, device_id_type=MESH)

    def exchange_rows(index):
        return pl.ds(pl.multiple_of(index * EX, 16), EX)

    def shared_rows(core):
        return pl.ds(pl.multiple_of(4 * EX + core * SHARED, 16), SHARED)

    own = 2 * e + c
    others = [lax.rem(own + i, 4) for i in (1, 2, 3)]
    enc = [exchange_rows(own), shared_rows(c)] + [exchange_rows(i) for i in others] + [shared_rows(1 - c)]
    moves = [(enc_ref.at[0, rows], mem.at[0, rows]) for rows in enc]
    moves.insert(1, (dec_ref.at[0, 0], dec.at[t]))
    moves += [(wk_ref.at[0], wkv.at[0]), (wv_ref.at[0], wkv.at[1]), (wq_ref.at[0], wq), (wo_ref.at[0], wo)]
    loads = [pltpu.make_async_copy(src, dst, local_sems.at[i]) for i, (src, dst) in enumerate(moves)]
    for copy in loads:
        copy.start()

    def normalize(hidden, factor):
        values = hidden.astype(F32)
        mean_sq = jnp.sum(values * values, axis=-1, keepdims=True) * (1.0 / width)
        return (values * lax.rsqrt(mean_sq + 1e-06) * factor).astype(BF16)

    def normalize_rows(start, size):
        def group(i, carry):
            rows = pl.ds(pl.multiple_of(start + i * 16, 16), 16)
            mem[0, rows, :] = normalize(mem[0, rows, :], gain[...])
            return carry

        lax.fori_loop(0, size // 16, group, 0)

    gain[...] = enc_gain_ref[...].reshape(1, width).astype(F32)
    loads[0].wait()
    normalize_rows(own * EX, EX)
    loads[1].wait()
    dec[t] = normalize(dec[t], dec_gain_ref[...].astype(F32))

    pl.semaphore_wait(barrier, 3 + (z < last).astype(jnp.int32) + (z > 0).astype(jnp.int32))

    pending = []

    def send(src, dst, recv_sem, target, when=None):
        copy = pltpu.make_async_remote_copy(
            src_ref=src,
            dst_ref=dst,
            send_sem=send_sems.at[len(pending)],
            recv_sem=recv_sem,
            device_id=target,
            device_id_type=MESH,
        )
        pending.append((copy, when))
        if when is None:
            copy.start()
        else:
            pl.when(when)(copy.start)

    def arrived(dst, recv_sem):
        pltpu.make_async_remote_copy(
            src_ref=dst,
            dst_ref=dst,
            send_sem=send_sems.at[0],
            recv_sem=recv_sem,
            device_id=other_core,
            device_id_type=MESH,
        ).wait_recv()

    def piece_rows(piece, parity, core):
        if piece == 0:
            start, size = (2 * parity + core) * EX, EX
        elif piece == 1:
            start, size = 4 * EX + core * SHARED, B1
        else:
            start, size = 4 * EX + core * SHARED + B1 + (piece - 2) * B2, B2
        return pl.ds(pl.multiple_of(start, 16), size)

    def to_x(slot, piece):
        rows = piece_rows(piece, e, c)
        send(
            mem.at[0, rows],
            mem.at[slot, rows],
            x_sems.at[slot, piece],
            section_up if slot == 2 else section_down,
        )

    to_x(2, 0)
    to_x(1, 0)
    send(dec.at[t], dec.at[t], dec_sems.at[0, 1], z_up, z < last)
    send(dec.at[t], dec.at[t], dec_sems.at[1, 1], z_down, z > 0)
    send(dec.at[t], dec.at[t], dec_core_sems.at[0, 0], other_core)
    loads[2].wait()
    normalize_rows(4 * EX + c * SHARED, SHARED)
    to_x(2, 2)
    to_x(1, 1)
    to_x(1, 2)
    to_x(2, 3)
    to_x(2, 1)

    def from_x(slot, piece):
        block = mem.at[slot, piece_rows(piece, e, c)]
        arrived(block, x_sems.at[slot, piece])
        if slot == 1 and piece in (0, 1):
            target = mem.at[3, piece_rows(piece, e, c)]
            send(block, target, x_sems.at[3, piece], section_down)
        if slot == 2 and piece in (2, 3):
            target = mem.at[3, piece_rows(piece, e, c)]
            send(block, target, x_sems.at[3, piece], section_up)
        if piece == 0:
            send(block, block, z_sems.at[slot], z_partner)
        send(block, block, core_sems.at[slot, piece], other_core)

    def from_z(slot):
        block = mem.at[slot, piece_rows(0, 1 - e, c)]
        arrived(block, z_sems.at[slot])
        send(block, block, core_sems.at[slot, 4], other_core)

    def from_core(slot, pieces):
        for piece in pieces:
            parity = 1 - e if piece == 4 else e
            arrived(mem.at[slot, piece_rows(piece % 4, parity, 1 - c)], core_sems.at[slot, piece])

    def from_decoder(k):
        below = z - k >= 0
        source = dec.at[jnp.maximum(t - 2 * k, 0)]

        @pl.when(below)
        def _():
            arrived(source, dec_sems.at[0, k])

        if k < last:
            send(source, source, dec_sems.at[0, k + 1], z_up, below & (z < last))
        send(source, source, dec_core_sems.at[0, k], other_core, below)
        above = z + k <= last
        source_ = dec.at[jnp.minimum(t + 2 * k, 2 * chips - 1)]

        @pl.when(above)
        def _():
            arrived(source_, dec_sems.at[1, k])

        if k < last:
            send(source_, source_, dec_sems.at[1, k + 1], z_down, above & (z > 0))
        send(source_, source_, dec_core_sems.at[1, k], other_core, above)

    def decoder_from_core():
        arrived(dec.at[t + 1 - 2 * c], dec_core_sems.at[0, 0])
        for k in range(1, chips):

            @pl.when(z - k >= 0)
            def _():
                source = dec.at[jnp.maximum(t - 2 * k + 1 - 2 * c, 0)]
                arrived(source, dec_core_sems.at[0, k])

            @pl.when(z + k <= last)
            def _():
                source = dec.at[jnp.minimum(t + 2 * k + 1 - 2 * c, 2 * chips - 1)]
                arrived(source, dec_core_sems.at[1, k])

    def project(slot, start, size):
        def side(n, carry):
            block = mem[slot, start : start + size, :]
            projected = jnp.dot(block, wkv[n], preferred_element_type=F32)
            kv[n, slot, start : start + size, :] = projected.astype(BF16)
            return carry

        lax.fori_loop(0, 2, side, 0)

    blocks = mem.shape[1]
    tokens = 2 * chips * dec.shape[1]

    def scores_of(slot, rows):
        scores = lax.dot_general(
            query[rows, :], kv[0, slot], (((1,), (1,)), ((), ())), preferred_element_type=F32
        )
        exponent = jnp.exp(scores)
        return exponent, jnp.sum(exponent, axis=-1, keepdims=True)

    def score(slot):
        exponent, row_sum = scores_of(slot, pl.ds(0, tokens))
        expo[slot] = exponent
        return row_sum

    for i, index in enumerate(others):
        loads[3 + i].wait()
        normalize_rows(index * EX, EX)
    loads[6].wait()
    normalize_rows(4 * EX + (1 - c) * SHARED, SHARED)
    from_decoder(1)
    from_x(1, 0)
    to_x(1, 3)
    from_x(2, 0)
    if chips > 2:
        from_decoder(2)
    loads[7].wait()
    loads[8].wait()
    project(0, 0, blocks)
    from_x(1, 1)
    if chips > 3:
        from_decoder(3)
    from_x(2, 2)
    from_x(1, 2)
    if chips > 4:
        from_decoder(4)
    from_x(2, 3)
    from_x(2, 1)
    from_x(3, 0)
    from_z(1)
    from_z(2)
    if chips > 5:
        from_decoder(5)
    decoder_from_core()
    loads[9].wait()
    queries = jnp.dot(dec[...].reshape(tokens, width), wq[...], preferred_element_type=F32)
    query[...] = queries.astype(BF16)
    total[...] = score(0)
    from_core(2, range(5))
    project(2, 0, blocks)
    from_x(1, 3)
    from_x(3, 2)
    from_z(3)
    total[...] += score(2)
    from_core(1, range(5))
    project(1, 0, blocks)
    from_x(3, 1)
    total[...] += score(1)
    from_core(3, (0, 4))
    project(3, 0, 4 * EX)
    from_x(3, 3)
    from_core(3, (1, 2, 3))
    project(3, 4 * EX, blocks - 4 * EX)
    loads[10].wait()

    def attend(start, size):
        rows = pl.ds(pl.multiple_of(start, 16), size)
        exponent, row_sum = scores_of(3, rows)
        inverse = 1.0 / (total[rows, :] + row_sum)
        attention = (exponent * inverse).astype(BF16)
        attended = jnp.dot(attention, kv[1, 3], preferred_element_type=F32)
        for slot in range(3):
            attention = (expo[slot, rows, :] * inverse).astype(BF16)
            attended += jnp.dot(attention, kv[1, slot], preferred_element_type=F32)
        attended = attended.astype(BF16)
        tile = min(512, width)
        share = dec.shape[1]
        for n in range(width // tile):
            columns = pl.ds(n * tile, tile)
            product = jnp.dot(attended, wo[:, columns], preferred_element_type=F32)
            part[pl.ds(start // share, size // share), :, columns] = product.reshape(size // share, share, tile)

    first = (z >= chips // 2).astype(jnp.int32)

    def line(direction, k):
        position = jnp.where(direction == 0, z, last - z)
        dest = jnp.where(direction == 0, last - k, k)
        return position, dest

    pair = []

    def swap(k):
        _, dest = line(first, k)
        to_core[dest] = part[2 * dest + 1 - c].astype(BF16)
        copy = pltpu.make_async_remote_copy(
            src_ref=to_core.at[dest],
            dst_ref=from_core_rows.at[dest],
            send_sem=pair_sems.at[0, k],
            recv_sem=pair_sems.at[1, k],
            device_id=other_core,
            device_id_type=MESH,
        )
        copy.start()
        pair.append(copy)

    piece_width = width // SPLIT
    sent = []

    def pass_on(direction, k):
        position, dest = line(direction, k)
        active = last - k > position
        for h in range(SPLIT):
            columns = pl.ds(h * piece_width, piece_width)
            landed = from_line.at[direction, dest, h]
            copy = pltpu.make_async_remote_copy(
                src_ref=to_line.at[direction, dest, h],
                dst_ref=landed,
                send_sem=line_send_sems.at[direction, k, h],
                recv_sem=line_sems.at[direction, k, h],
                device_id={"tensor": t + 2 - 4 * direction},
                device_id_type=MESH,
            )
            mine = lambda: part[2 * dest + c, :, columns] + from_core_rows[dest, :, columns].astype(F32)

            @pl.when(active & (position == 0))
            def _():
                to_line[direction, dest, h] = mine().astype(BF16)
                copy.start()

            @pl.when(active & (position > 0))
            def _():
                arrived(landed, line_sems.at[direction, k, h])
                value = mine() + from_line[direction, dest, h].astype(F32)
                to_line[direction, dest, h] = value.astype(BF16)
                copy.start()

            sent.append((copy, active))

    half = tokens // 2
    far = half * (1 - first)
    attend(far, half)
    for k in range(chips // 2):
        swap(k)
    pair[0].wait_recv()
    pass_on(first, 0)
    attend(half - far, half)
    for k in range(chips // 2, chips):
        swap(k)
    for k in range(1, chips):
        pair[k].wait_recv()
        if k < last:
            pass_on(first, k)
    for k in range(last - (chips + 1) // 2):
        pass_on(1 - first, k)

    for h in range(SPLIT):
        columns = pl.ds(h * piece_width, piece_width)
        part[t, :, columns] += from_core_rows[z, :, columns].astype(F32)

        @pl.when(z > 0)
        def _():
            arrived(from_line.at[0, z, h], line_sems.at[0, last - z, h])
            part[t, :, columns] += from_line[0, z, h].astype(F32)

        @pl.when(z < last)
        def _():
            arrived(from_line.at[1, z, h], line_sems.at[1, z, h])
            part[t, :, columns] += from_line[1, z, h].astype(F32)

        out_ref[:, columns] = part[t, :, columns].astype(BF16)

    for copy, when in pending + sent:
        if when is None:
            copy.wait_send()
        else:
            pl.when(when)(copy.wait_send)
    for copy in pair:
        copy.wait_send()


def body(enc_hidden, dec_hidden, enc_gain, dec_gain, w_query, w_key, w_value, w_out):
    chips = lax.axis_size("tensor") // 2
    rows, width = enc_hidden.shape[1:]
    share = dec_hidden.shape[2]
    head = w_query.shape[2]
    any_space = pl.BlockSpec(memory_space=pl.ANY)
    vmem = pl.BlockSpec(memory_space=pltpu.VMEM)
    dma = pltpu.SemaphoreType.DMA
    mixed = pl.pallas_call(
        functools.partial(kernel, chips),
        out_shape=jax.ShapeDtypeStruct((share, width), BF16),
        in_specs=[any_space, any_space, vmem, vmem] + [any_space] * 4,
        out_specs=vmem,
        scratch_shapes=[
            pltpu.VMEM((4, rows, width), BF16),
            pltpu.VMEM((2 * chips, share, width), BF16),
            pltpu.VMEM((width, head), BF16),
            pltpu.VMEM((2, width, head), BF16),
            pltpu.VMEM((head, width), BF16),
            pltpu.VMEM((1, width), F32),
            pltpu.VMEM((2 * chips * share, head), BF16),
            pltpu.VMEM((2 * chips * share, 1), F32),
            pltpu.VMEM((2, 4, rows, head), BF16),
            pltpu.VMEM((4, 2 * chips * share, rows), F32),
            pltpu.VMEM((2 * chips, share, width), F32),
            pltpu.VMEM((chips, share, width), BF16),
            pltpu.VMEM((chips, share, width), BF16),
            pltpu.VMEM((2, chips, SPLIT, share, width // SPLIT), BF16),
            pltpu.VMEM((2, chips, SPLIT, share, width // SPLIT), BF16),
            dma((64,)),
            dma((11,)),
            dma((4, 4)),
            dma((4,)),
            dma((4, 5)),
            dma((2, chips + 1)),
            dma((2, chips)),
            dma((2, chips)),
            dma((2, chips, SPLIT)),
            dma((2, chips, SPLIT)),
        ],
        compiler_params=pltpu.CompilerParams(
            collective_id=0, has_side_effects=True, vmem_limit_bytes=60 * 1024 * 1024
        ),
        name="cross_attention",
    )(
        enc_hidden,
        dec_hidden,
        enc_gain,
        dec_gain,
        w_query,
        w_key,
        w_value,
        w_out,
    )
    return mixed[None, None]


def solution(mesh):
    return jax.shard_map(
        body,
        mesh=mesh,
        in_specs=(
            P("dp", "section", None),
            P("section", "dp", "tensor", None),
            P(),
            P("section", None),
            P("section", None, "tensor"),
            P("section", None, "tensor"),
            P("section", None, "tensor"),
            P("section", "tensor", None),
        ),
        out_specs=P("section", "dp", "tensor", None),
        check_vma=False,
    )
```

```python
import functools

import jax
import jax.numpy as jnp
from jax import lax
from jax.experimental import pallas as pl
from jax.experimental.pallas import tpu as pltpu
from jax.sharding import PartitionSpec as P

F32 = jnp.float32
BF16 = jnp.bfloat16
MESH = pl.DeviceIdType.MESH

EX = 32
B1 = 16
B2 = 32
SHARED = B1 + 2 * B2
SPLIT = 4


def kernel(
    chips,
    enc_ref,
    dec_ref,
    enc_gain_ref,
    dec_gain_ref,
    wq_ref,
    wk_ref,
    wv_ref,
    wo_ref,
    out_ref,
    mem,
    dec,
    wq,
    wkv,
    wo,
    gain,
    query,
    total,
    kv,
    expo,
    part,
    to_core,
    from_core_rows,
    to_line,
    from_line,
    send_sems,
    local_sems,
    x_sems,
    z_sems,
    core_sems,
    dec_sems,
    dec_core_sems,
    pair_sems,
    line_sems,
    line_send_sems,
):
    sections = lax.axis_size("section")
    s = lax.axis_index("section")
    t = lax.axis_index("tensor")
    z = t // 2
    c = t % 2
    e = z % 2
    last = chips - 1
    width = mem.shape[2]
    section_up = {"section": lax.rem(s + 1, sections)}
    section_down = {"section": lax.rem(s + sections - 1, sections)}
    other_core = {"tensor": t + 1 - 2 * c}
    z_partner = {"tensor": t + 2 - 4 * e}
    z_up = {"tensor": t + 2}
    z_down = {"tensor": t - 2}

    barrier = pltpu.get_barrier_semaphore()
    for target in (section_up, section_down, other_core):
        pl.semaphore_signal(barrier, inc=1, device_id=target, device_id_type=MESH)

    @pl.when(z < last)
    def _():
        pl.semaphore_signal(barrier, inc=1, device_id=z_up, device_id_type=MESH)

    @pl.when(z > 0)
    def _():
        pl.semaphore_signal(barrier, inc=1, device_id=z_down, device_id_type=MESH)

    def piece_rows(piece, parity, core):
        if piece == 0:
            start, size = (2 * parity + core) * EX, EX
        elif piece == 2:
            start, size = 4 * EX + core * B2, B2
        elif piece == 1:
            start, size = 4 * EX + 2 * B2 + core * B1, B1
        else:
            start, size = 4 * EX + 2 * B2 + 2 * B1 + core * B2, B2
        return pl.ds(pl.multiple_of(start, 16), size)

    def exchange_rows(index):
        return pl.ds(pl.multiple_of(index * EX, 16), EX)

    own = 2 * e + c
    others = [lax.rem(own + i, 4) for i in (1, 2, 3)]
    enc = [exchange_rows(own), pl.ds(4 * EX, 2 * SHARED)] + [exchange_rows(i) for i in others]
    moves = [(enc_ref.at[0, rows], mem.at[0, rows]) for rows in enc]
    moves.insert(1, (dec_ref.at[0, 0], dec.at[t]))
    moves += [(wk_ref.at[0], wkv.at[0]), (wv_ref.at[0], wkv.at[1]), (wq_ref.at[0], wq), (wo_ref.at[0], wo)]
    loads = [pltpu.make_async_copy(src, dst, local_sems.at[i]) for i, (src, dst) in enumerate(moves)]
    for copy in loads:
        copy.start()

    def normalize(hidden, factor):
        values = hidden.astype(F32)
        mean_sq = jnp.sum(values * values, axis=-1, keepdims=True) * (1.0 / width)
        return (values * lax.rsqrt(mean_sq + 1e-06) * factor).astype(BF16)

    def normalize_rows(rows):
        start, size = rows.start, rows.size

        def group(i, carry):
            rows = pl.ds(pl.multiple_of(start + i * 16, 16), 16)
            mem[0, rows, :] = normalize(mem[0, rows, :], gain[...])
            return carry

        lax.fori_loop(0, size // 16, group, 0)

    gain[...] = enc_gain_ref[...].reshape(1, width).astype(F32)
    loads[0].wait()
    normalize_rows(exchange_rows(own))
    loads[1].wait()
    dec[t] = normalize(dec[t], dec_gain_ref[...].astype(F32))

    pl.semaphore_wait(barrier, 3 + (z < last).astype(jnp.int32) + (z > 0).astype(jnp.int32))

    pending = []

    def send(src, dst, recv_sem, target, when=None):
        copy = pltpu.make_async_remote_copy(
            src_ref=src,
            dst_ref=dst,
            send_sem=send_sems.at[len(pending)],
            recv_sem=recv_sem,
            device_id=target,
            device_id_type=MESH,
        )
        pending.append((copy, when))
        if when is None:
            copy.start()
        else:
            pl.when(when)(copy.start)

    def arrived(dst, recv_sem):
        pltpu.make_async_remote_copy(
            src_ref=dst,
            dst_ref=dst,
            send_sem=send_sems.at[0],
            recv_sem=recv_sem,
            device_id=other_core,
            device_id_type=MESH,
        ).wait_recv()

    def to_x(slot, piece):
        rows = piece_rows(piece, e, c)
        send(
            mem.at[0, rows],
            mem.at[slot, rows],
            x_sems.at[slot, piece],
            section_up if slot == 2 else section_down,
        )

    to_x(2, 0)
    to_x(1, 0)
    send(dec.at[t], dec.at[t], dec_sems.at[0, 1], z_up, z < last)
    send(dec.at[t], dec.at[t], dec_sems.at[1, 1], z_down, z > 0)
    send(dec.at[t], dec.at[t], dec_core_sems.at[0, 0], other_core)
    loads[2].wait()
    normalize_rows(piece_rows(2, e, c))
    to_x(2, 2)
    normalize_rows(piece_rows(1, e, c))
    to_x(1, 1)
    normalize_rows(piece_rows(3, e, c))
    to_x(2, 3)
    to_x(2, 1)

    def from_x(slot, piece):
        block = mem.at[slot, piece_rows(piece, e, c)]
        arrived(block, x_sems.at[slot, piece])
        if slot == 1 and piece in (0, 1):
            target = mem.at[3, piece_rows(piece, e, c)]
            send(block, target, x_sems.at[3, piece], section_down)
        if slot == 2 and piece in (2, 3):
            target = mem.at[3, piece_rows(piece, e, c)]
            send(block, target, x_sems.at[3, piece], section_up)
        if piece == 0:
            send(block, block, z_sems.at[slot], z_partner)
        send(block, block, core_sems.at[slot, piece], other_core)

    def from_z(slot):
        block = mem.at[slot, piece_rows(0, 1 - e, c)]
        arrived(block, z_sems.at[slot])
        send(block, block, core_sems.at[slot, 4], other_core)

    def from_core(slot, pieces):
        for piece in pieces:
            parity = 1 - e if piece == 4 else e
            arrived(mem.at[slot, piece_rows(piece % 4, parity, 1 - c)], core_sems.at[slot, piece])

    def from_decoder(k):
        below = z - k >= 0
        source = dec.at[jnp.maximum(t - 2 * k, 0)]

        @pl.when(below)
        def _():
            arrived(source, dec_sems.at[0, k])

        if k < last:
            send(source, source, dec_sems.at[0, k + 1], z_up, below & (z < last))
        send(source, source, dec_core_sems.at[0, k], other_core, below)
        above = z + k <= last
        source_ = dec.at[jnp.minimum(t + 2 * k, 2 * chips - 1)]

        @pl.when(above)
        def _():
            arrived(source_, dec_sems.at[1, k])

        if k < last:
            send(source_, source_, dec_sems.at[1, k + 1], z_down, above & (z > 0))
        send(source_, source_, dec_core_sems.at[1, k], other_core, above)

    def decoder_from_core():
        arrived(dec.at[t + 1 - 2 * c], dec_core_sems.at[0, 0])
        for k in range(1, chips):

            @pl.when(z - k >= 0)
            def _():
                source = dec.at[jnp.maximum(t - 2 * k + 1 - 2 * c, 0)]
                arrived(source, dec_core_sems.at[0, k])

            @pl.when(z + k <= last)
            def _():
                source = dec.at[jnp.minimum(t + 2 * k + 1 - 2 * c, 2 * chips - 1)]
                arrived(source, dec_core_sems.at[1, k])

    def project(slot, start, size):
        def side(n, carry):
            block = mem[slot, start : start + size, :]
            projected = jnp.dot(block, wkv[n], preferred_element_type=F32)
            kv[n, slot, start : start + size, :] = projected.astype(BF16)
            return carry

        lax.fori_loop(0, 2, side, 0)

    blocks = mem.shape[1]
    tokens = 2 * chips * dec.shape[1]

    def scores_of(slot, rows):
        scores = lax.dot_general(
            query[rows, :], kv[0, slot], (((1,), (1,)), ((), ())), preferred_element_type=F32
        )
        exponent = jnp.exp(scores)
        return exponent, jnp.sum(exponent, axis=-1, keepdims=True)

    def score(slot):
        exponent, row_sum = scores_of(slot, pl.ds(0, tokens))
        expo[slot] = exponent
        return row_sum

    for i, index in enumerate(others):
        loads[3 + i].wait()
        normalize_rows(exchange_rows(index))
    from_decoder(1)
    from_x(1, 0)
    to_x(1, 2)
    to_x(1, 3)
    from_x(2, 0)
    for piece in (1, 2, 3):
        normalize_rows(piece_rows(piece, e, 1 - c))
    if chips > 2:
        from_decoder(2)
    loads[6].wait()
    loads[7].wait()
    project(0, 0, blocks)
    from_x(1, 1)
    if chips > 3:
        from_decoder(3)
    from_x(2, 2)
    from_x(3, 0)
    if chips > 4:
        from_decoder(4)
    from_x(2, 3)
    from_z(1)
    from_x(2, 1)
    from_z(2)
    if chips > 5:
        from_decoder(5)
    decoder_from_core()
    loads[8].wait()
    queries = jnp.dot(dec[...].reshape(tokens, width), wq[...], preferred_element_type=F32)
    query[...] = queries.astype(BF16)
    total[...] = score(0)
    from_x(1, 2)
    from_core(2, range(5))
    project(2, 0, blocks)
    total[...] += score(2)
    from_x(1, 3)
    from_x(3, 2)
    from_core(1, range(5))
    project(1, 0, blocks)
    total[...] += score(1)
    from_core(3, (2,))
    project(3, 4 * EX, 2 * B2)
    from_z(3)
    from_x(3, 1)
    from_x(3, 3)
    from_core(3, (0, 4))
    project(3, 0, 4 * EX)
    from_core(3, (1, 3))
    project(3, 4 * EX + 2 * B2, 2 * B1 + 2 * B2)
    loads[9].wait()

    def attend(start, size):
        rows = pl.ds(pl.multiple_of(start, 16), size)
        exponent, row_sum = scores_of(3, rows)
        inverse = 1.0 / (total[rows, :] + row_sum)
        attention = (exponent * inverse).astype(BF16)
        attended = jnp.dot(attention, kv[1, 3], preferred_element_type=F32)
        for slot in range(3):
            attention = (expo[slot, rows, :] * inverse).astype(BF16)
            attended += jnp.dot(attention, kv[1, slot], preferred_element_type=F32)
        attended = attended.astype(BF16)
        tile = min(512, width)
        share = dec.shape[1]
        for n in range(width // tile):
            columns = pl.ds(n * tile, tile)
            product = jnp.dot(attended, wo[:, columns], preferred_element_type=F32)
            part[pl.ds(start // share, size // share), :, columns] = product.reshape(size // share, share, tile)

    first = (z >= chips // 2).astype(jnp.int32)

    def line(direction, k):
        position = jnp.where(direction == 0, z, last - z)
        dest = jnp.where(direction == 0, last - k, k)
        return position, dest

    pair = []

    def swap(k):
        _, dest = line(first, k)
        to_core[dest] = part[2 * dest + 1 - c].astype(BF16)
        copy = pltpu.make_async_remote_copy(
            src_ref=to_core.at[dest],
            dst_ref=from_core_rows.at[dest],
            send_sem=pair_sems.at[0, k],
            recv_sem=pair_sems.at[1, k],
            device_id=other_core,
            device_id_type=MESH,
        )
        copy.start()
        pair.append(copy)

    piece_width = width // SPLIT
    sent = []

    def pass_on(direction, k, only=None):
        position, dest = line(direction, k)
        active = last - k > position
        if only is not None:
            active &= position == only
        for h in range(SPLIT):
            columns = pl.ds(h * piece_width, piece_width)
            landed = from_line.at[direction, dest, h]
            copy = pltpu.make_async_remote_copy(
                src_ref=to_line.at[direction, dest, h],
                dst_ref=landed,
                send_sem=line_send_sems.at[direction, k, h],
                recv_sem=line_sems.at[direction, k, h],
                device_id={"tensor": t + 2 - 4 * direction},
                device_id_type=MESH,
            )
            mine = lambda: part[2 * dest + c, :, columns] + from_core_rows[dest, :, columns].astype(F32)

            @pl.when(active & (position == 0))
            def _():
                to_line[direction, dest, h] = mine().astype(BF16)
                copy.start()

            @pl.when(active & (position > 0))
            def _():
                arrived(landed, line_sems.at[direction, k, h])
                value = mine() + from_line[direction, dest, h].astype(F32)
                to_line[direction, dest, h] = value.astype(BF16)
                copy.start()

            sent.append((copy, active))

    half = tokens // 2
    far = half * (1 - first)
    attend(far, half)
    for k in range(chips // 2):
        swap(k)
    pair[0].wait_recv()
    pass_on(first, 0)
    attend(half - far, half)
    for k in range(chips // 2, chips):
        swap(k)
    for k in range(1, chips):
        pair[k].wait_recv()

    for step in range(1, last):
        pass_on(first, step)
        for i in range(1, chips // 2):
            k = step - last + 2 * i
            if 0 <= k < i:
                pass_on(1 - first, k, last - i)

    for h in range(SPLIT):
        columns = pl.ds(h * piece_width, piece_width)
        part[t, :, columns] += from_core_rows[z, :, columns].astype(F32)

        @pl.when(z > 0)
        def _():
            arrived(from_line.at[0, z, h], line_sems.at[0, last - z, h])
            part[t, :, columns] += from_line[0, z, h].astype(F32)

        @pl.when(z < last)
        def _():
            arrived(from_line.at[1, z, h], line_sems.at[1, z, h])
            part[t, :, columns] += from_line[1, z, h].astype(F32)

        out_ref[:, columns] = part[t, :, columns].astype(BF16)

    for copy, when in pending + sent:
        if when is None:
            copy.wait_send()
        else:
            pl.when(when)(copy.wait_send)
    for copy in pair:
        copy.wait_send()


def body(enc_hidden, dec_hidden, enc_gain, dec_gain, w_query, w_key, w_value, w_out):
    chips = lax.axis_size("tensor") // 2
    rows, width = enc_hidden.shape[1:]
    share = dec_hidden.shape[2]
    head = w_query.shape[2]
    any_space = pl.BlockSpec(memory_space=pl.ANY)
    vmem = pl.BlockSpec(memory_space=pltpu.VMEM)
    dma = pltpu.SemaphoreType.DMA
    mixed = pl.pallas_call(
        functools.partial(kernel, chips),
        out_shape=jax.ShapeDtypeStruct((share, width), BF16),
        in_specs=[any_space, any_space, vmem, vmem] + [any_space] * 4,
        out_specs=vmem,
        scratch_shapes=[
            pltpu.VMEM((4, rows, width), BF16),
            pltpu.VMEM((2 * chips, share, width), BF16),
            pltpu.VMEM((width, head), BF16),
            pltpu.VMEM((2, width, head), BF16),
            pltpu.VMEM((head, width), BF16),
            pltpu.VMEM((1, width), F32),
            pltpu.VMEM((2 * chips * share, head), BF16),
            pltpu.VMEM((2 * chips * share, 1), F32),
            pltpu.VMEM((2, 4, rows, head), BF16),
            pltpu.VMEM((4, 2 * chips * share, rows), F32),
            pltpu.VMEM((2 * chips, share, width), F32),
            pltpu.VMEM((chips, share, width), BF16),
            pltpu.VMEM((chips, share, width), BF16),
            pltpu.VMEM((2, chips, SPLIT, share, width // SPLIT), BF16),
            pltpu.VMEM((2, chips, SPLIT, share, width // SPLIT), BF16),
            dma((64,)),
            dma((11,)),
            dma((4, 4)),
            dma((4,)),
            dma((4, 5)),
            dma((2, chips + 1)),
            dma((2, chips)),
            dma((2, chips)),
            dma((2, chips, SPLIT)),
            dma((2, chips, SPLIT)),
        ],
        compiler_params=pltpu.CompilerParams(
            collective_id=0, has_side_effects=True, vmem_limit_bytes=60 * 1024 * 1024
        ),
        name="cross_attention",
    )(
        enc_hidden,
        dec_hidden,
        enc_gain,
        dec_gain,
        w_query,
        w_key,
        w_value,
        w_out,
    )
    return mixed[None, None]


def solution(mesh):
    return jax.shard_map(
        body,
        mesh=mesh,
        in_specs=(
            P("dp", "section", None),
            P("section", "dp", "tensor", None),
            P(),
            P("section", None),
            P("section", None, "tensor"),
            P("section", None, "tensor"),
            P("section", None, "tensor"),
            P("section", "tensor", None),
        ),
        out_specs=P("section", "dp", "tensor", None),
        check_vma=False,
    )
```
